256 devices in a mesh: chain: 16 (over z, core), bond: 16 (over y, x).
Axes of the slice: x: 4, y: 4, z: 8, core: 2. Of those that a mesh axis runs over, the one named last changes fastest.
Arguments:
- site_tensors: float32 [64, 256, 2, 256], P('chain', 'bond'), may hold values from -20 to 20
- bond_gates: float32 [64, 4, 4], P('chain'), may hold values from -1.5 to 2.5
Outputs:
- state: float32 [64, 256, 2, 256], P('chain', 'bond')
- profile: float32 [64], P('chain')
The draws below stay inside these ranges and needn't reach their ends.
All inputs are finite; a program needn't handle non-finite values.
Results may differ from the reference program's by a relative error of at most 0.0002.
Values sent between devices are 32-bit elements; how exact they have to be, the bound alone decides.
No kernel may reach another device: no remote copies, remote signals or barrier semaphores. Data moves between devices by JAX's collectives and lax.ppermute only.
A program may use at most 64 MiB of HBM per device.

```python
import math
import jax
import jax.numpy as jnp
from jax import lax

CHI = 256
NS_ITERS = 3
SITES = 64


def draw_site_tensors(key, part):
    key_base = jax.random.fold_in(key, 11)
    shape = (SITES, CHI, 2, CHI)
    base = jnp.clip(jax.random.normal(key_base, shape, jnp.float32), -6.0, 6.0)
    ramp = jnp.exp(-2.0 * jnp.arange(SITES, dtype=jnp.float32) / SITES)
    return base * ramp[:, None, None, None]


def draw_bond_gates(key, part):
    key_noise = jax.random.fold_in(key, 21)
    noise = 0.3 * jnp.clip(jax.random.normal(key_noise, (SITES, 4, 4), jnp.float32), -4.0, 4.0)
    return jnp.eye(4, dtype=jnp.float32)[None, :, :] + noise


def setup_inputs(seed: int = 0) -> dict:
    key_list = jax.random.split(jax.random.key(seed), 3)
    return {
        "site_tensors": draw_site_tensors(jax.random.fold_in(key_list[2], 71), 0),
        "bond_gates": draw_bond_gates(jax.random.fold_in(key_list[2], 71), 0),
    }


epsilon = 1e-06
exact = lax.Precision.HIGHEST

def bond_update(operands):
    left, right, gate = operands
    width = left.shape[0]
    two_site = jnp.einsum('asm,mtb->astb', left, right, precision=exact) / math.sqrt(width)
    gated = jnp.einsum('stuv,auvb->astb', gate.reshape(2, 2, 2, 2), two_site, precision=exact)
    matrix = gated.reshape(2 * width, 2 * width)
    projected = jnp.dot(matrix, right.reshape(width, 2 * width).T, precision=exact)
    squares = jnp.sum(projected * projected)
    iterate = projected / jnp.sqrt(squares + epsilon)
    for repeat in range(NS_ITERS):
        gram = jnp.dot(iterate.T, iterate, precision=exact)
        iterate = 1.5 * iterate - 0.5 * jnp.dot(iterate, gram, precision=exact)
    carried = jnp.dot(iterate.T, matrix, precision=exact)
    scale_norm = jnp.sqrt(jnp.mean(carried * carried) + epsilon)
    new_left = (math.sqrt(2 * width) * iterate).reshape(width, 2, width)
    new_right = (carried / scale_norm).reshape(width, 2, width)
    return (new_left, new_right, jnp.log(scale_norm))

def reference(site_tensors, bond_gates):
    sites = site_tensors.shape[0]
    new_left, new_right, weights_even = lax.map(bond_update, (site_tensors[0::2], site_tensors[1::2], bond_gates[0::2]))
    half_state = jnp.stack([new_left, new_right], axis=1).reshape(site_tensors.shape)
    rolled = jnp.roll(half_state, -1, axis=0)
    new_left, new_right, weights_odd = lax.map(bond_update, (half_state[1::2], rolled[1::2], bond_gates[1::2]))
    even_sites = jnp.roll(new_right, 1, axis=0)
    state = jnp.stack([even_sites, new_left], axis=1).reshape(site_tensors.shape)
    weights = jnp.stack([weights_even, weights_odd], axis=1).reshape(sites)
    profile = jnp.cumsum(weights) / sites
    return (state, profile)
```

```python
import math

import jax
import jax.numpy as jnp
from jax import lax
from jax.experimental import pallas as pl
from jax.experimental.pallas import tpu as pltpu
from jax.sharding import Mesh, PartitionSpec as P

EPS = 1e-06
F32, BF16 = jnp.float32, jnp.bfloat16
ROWS_CHUNK = 16


def halves(value):
    high = value.astype(BF16)
    return high, (value - high.astype(F32)).astype(BF16)


def put(high_ref, low_ref, at, value):
    high_ref[at], low_ref[at] = halves(value)


def product(lefts, rights, transposed=False):
    lhs = jnp.concatenate([part for high, low in lefts for part in (high, high, low)], axis=1)
    axis = 1 if transposed else 0
    rhs = jnp.concatenate([part for high, low in rights for part in (high, low, high)], axis=axis)
    return lax.dot_general(lhs, rhs, (((1,), (axis,)), ((), ())), preferred_element_type=F32)


def two_site_matrix(gate_ref, site, left, right, theta, phi_high, phi_low):
    width = theta.shape[2]
    for t in range(2):
        both = product([left], [right[t]])
        theta[0, t], theta[1, t] = both[:width], both[width:]
    scale = 1.0 / math.sqrt(width)
    gate = [[gate_ref[site, i, j] * scale for j in range(4)] for i in range(4)]

    def chunk(k, _):
        at = pl.ds(pl.multiple_of(k * ROWS_CHUNK, ROWS_CHUNK), ROWS_CHUNK)
        parts = [theta[u, v, at] for u in range(2) for v in range(2)]
        for s in range(2):
            for t in range(2):
                row = gate[2 * s + t]
                mixed = row[0] * parts[0] + row[1] * parts[1] + (row[2] * parts[2] + row[3] * parts[3])
                put(phi_high, phi_low, (s, t, at), mixed)
        return 0

    lax.fori_loop(0, width // ROWS_CHUNK, chunk, 0, unroll=4)


def projected(right, phi_high, phi_low, flipped, flip_high, flip_low):
    for s in range(2):
        flipped[s] = product(right, [(phi_high[s, t], phi_low[s, t]) for t in range(2)], True)
        put(flip_high, flip_low, s, flipped[s])


def orthogonalizer(flipped, flip_high, flip_low):
    width = flipped.shape[1]
    total = jnp.sum(flipped[0] * flipped[0] + flipped[1] * flipped[1], axis=(0, 1), keepdims=True)
    norm = jnp.sqrt(total + EPS)
    pairs = [(flip_high[s], flip_low[s]) for s in range(2)]
    gram = product(pairs, pairs, True) * (1.0 / (total + EPS))
    rows = lax.broadcasted_iota(jnp.int32, (width, width), 0)
    columns = lax.broadcasted_iota(jnp.int32, (width, width), 1)
    unit = jnp.where(rows == columns, 1.0, 0.0).astype(F32)
    g = halves(gram)
    square = product([g], [g])
    a = halves(square)
    two = product([a], [halves(0.0625 * square - 0.5625 * gram)])
    two = two + (2.25 * unit - 2.4375 * gram + 1.6875 * square)
    w = halves(two)
    once = product([g], [w])
    twice = product([w], [w])
    three = 1.5 * two - 0.5 * product([halves(once)], [halves(twice)])
    return three * (1.0 / norm)


def carried_planes(p, flip_high, flip_low, phi_high, phi_low, carried):
    size = carried.shape[1] * carried.shape[2] * 2
    total = jnp.zeros((1, 1), F32)
    for t in range(2):
        mixed = product(
            [(flip_high[s], flip_low[s]) for s in range(2)],
            [(phi_high[s, t], phi_low[s, t]) for s in range(2)],
        )
        plane = product([p], [halves(mixed)])
        carried[t] = plane
        total = total + jnp.sum(plane * plane, axis=(0, 1), keepdims=True)
    return jnp.sqrt(total * (1.0 / size) + EPS)


def pair_of_bond():
    return lax.axis_index("xh") ^ lax.axis_index("c")


def even_first(
    got, gates, new_left, p_out, flip_high, flip_low, phi_high, phi_low, theta, flipped, left_high, left_low, right_high, right_low
):
    width = theta.shape[2]
    for s in range(2):
        put(left_high, left_low, pl.ds(s * width, width), got[:, 0, s].reshape(width, width))
        put(right_high, right_low, s, got[:, 1, s].reshape(width, width))
    right = [(right_high[t], right_low[t]) for t in range(2)]
    two_site_matrix(gates, 2 * pair_of_bond(), (left_high[...], left_low[...]), right, theta, phi_high, phi_low)
    projected(right, phi_high, phi_low, flipped, flip_high, flip_low)
    p = orthogonalizer(flipped, flip_high, flip_low)
    p_out[...] = p
    p = halves(p)
    for s in range(2):
        new_left[s] = math.sqrt(2 * width) * product([halves(flipped[s].T)], [p])


def even_second(p_in, flip_high, flip_low, phi_high, phi_low, new_right, weight):
    norm = carried_planes(halves(p_in[...]), flip_high, flip_low, phi_high, phi_low, new_right)
    for t in range(2):
        new_right[t] = new_right[t] * (1.0 / norm)
    weight[...] = jnp.broadcast_to(jnp.log(norm), weight.shape)


def odd_whole(
    left_in, right_in, gates, own_left, own_right, other, other_right, weight,
    theta, flipped, carried, flip_high, flip_low, phi_high, phi_low, left_high, left_low, right_high, right_low,
):
    width = theta.shape[2]
    depth = own_left.shape[1]
    for s in range(2):
        put(left_high, left_low, pl.ds(s * width, width), left_in[s])
        put(right_high, right_low, s, right_in[s])
    right = [(right_high[t], right_low[t]) for t in range(2)]
    two_site_matrix(gates, 2 * pair_of_bond() + 1, (left_high[...], left_low[...]), right, theta, phi_high, phi_low)
    projected(right, phi_high, phi_low, flipped, flip_high, flip_low)
    y, xh, xl = lax.axis_index("y"), lax.axis_index("xh"), lax.axis_index("xl")
    blocks = [pl.ds(pl.multiple_of(b * depth, depth), depth) for b in (4 * y + 2 * xh + xl, 4 * y + 2 * (1 - xh) + (1 - xl))]
    picked = [
        tuple(jnp.concatenate([ref[s, t, at] for at in blocks for s in range(2)], axis=0) for ref in (phi_high, phi_low))
        for t in range(2)
    ]
    some = product(picked, right, True)
    p = halves(orthogonalizer(flipped, flip_high, flip_low))
    norm = carried_planes(p, flip_high, flip_low, phi_high, phi_low, carried)
    weight[...] = jnp.broadcast_to(jnp.log(norm), weight.shape)
    some = math.sqrt(2 * width) * product([halves(some)], [p])
    inverse = 1.0 / norm
    for s in range(2):
        own_left[s] = some[s * depth : (s + 1) * depth]
        other[0, s] = some[(2 + s) * depth : (3 + s) * depth]
        own_right[s] = carried[s, blocks[0]] * inverse
        there = carried[s, blocks[1]] * inverse
        other[1, s] = there
        other_right[s] = there


def planes(width, dtype, *lead):
    return pltpu.VMEM((*lead, width, width), dtype)


def shaped(dtype, *shape):
    return jax.ShapeDtypeStruct(shape, dtype)


VMEM = pl.BlockSpec(memory_space=pltpu.VMEM)
SMEM = pl.BlockSpec(memory_space=pltpu.SMEM)
PARAMS = pltpu.CompilerParams(vmem_limit_bytes=24 << 20)


def cost(products, width):
    return pl.CostEstimate(flops=6 * products * width**3, bytes_accessed=1 << 21, transcendentals=0)


def per_device(site_tensors, bond_gates):
    sites, depth, spins, width = site_tensors.shape
    zs, ys = lax.axis_size("z"), lax.axis_size("y")
    c, xh = lax.axis_index("c"), lax.axis_index("xh")
    chain, bond = ("z", "c"), ("y", "xh", "xl")
    pair = xh ^ c
    split = [
        shaped(BF16, 2, width, width), shaped(BF16, 2, width, width),
        shaped(BF16, 2, 2, width, width), shaped(BF16, 2, 2, width, width),
    ]
    operands = [
        pltpu.VMEM((2 * width, width), BF16), pltpu.VMEM((2 * width, width), BF16),
        planes(width, BF16, 2), planes(width, BF16, 2),
    ]

    by_spin = jnp.swapaxes(site_tensors, 1, 2)
    by_spin = jnp.where(c == 0, by_spin, jnp.roll(by_spin, 2, axis=0)).reshape(2, 2, spins, depth, width)
    sent = jnp.broadcast_to(by_spin[None, :, None], (ys, 2, 2, 2, spins, depth, width))
    got = lax.all_to_all(sent.reshape(-1, 2, spins, depth, width), bond, 0, 0, tiled=True)

    new_left, p, *kept = pl.pallas_call(
        even_first,
        out_shape=[shaped(F32, 2, width, width), shaped(F32, width, width), *split],
        in_specs=[VMEM, SMEM],
        out_specs=[VMEM] * 6,
        scratch_shapes=[planes(width, F32, 2, 2), planes(width, F32, 2), *operands],
        compiler_params=PARAMS,
        cost_estimate=cost(17, width),
        name="even_first",
    )(got, bond_gates)

    def number(z, k, y, i, j):
        return (((z * 2 + k) * ys + y) * 2 + i) * 2 + j

    every = [(z, k, y, i, j) for z in range(zs) for k in range(2) for y in range(ys) for i in range(2) for j in range(2)]
    route, beside, onward, across = [], [], [], []
    for z, k, y, i, j in every:
        after = ((z + k) % zs, 1 - k)
        here = number(z, k, y, i, j)
        opposite = number(z, k, y, 1 - i, 1 - j)
        beside.append((here, opposite))
        if i ^ k:
            route.append((number(*after, y, i, j), here))
            onward.append((here, number(*after, y, i, j)))
            across.append((here, number(*after, y, 1 - i, 1 - j)))
        else:
            route.append((opposite, here))
    everywhere = chain + bond
    next_left = lax.ppermute(new_left, everywhere, route)

    new_right, even_weight = pl.pallas_call(
        even_second,
        out_shape=[shaped(F32, 2, width, width), shaped(F32, 8, 128)],
        in_specs=[VMEM] * 5,
        out_specs=[VMEM] * 2,
        compiler_params=PARAMS,
        cost_estimate=cost(6, width),
        name="even_second",
    )(p, *kept)

    block = (2, depth, width)
    own_left, own_right, other, other_right, odd_weight = pl.pallas_call(
        odd_whole,
        out_shape=[shaped(F32, *block), shaped(F32, *block), shaped(F32, 2, *block), shaped(F32, *block), shaped(F32, 8, 128)],
        in_specs=[VMEM, VMEM, SMEM],
        out_specs=[VMEM] * 5,
        scratch_shapes=[
            planes(width, F32, 2, 2), planes(width, F32, 2), planes(width, F32, 2),
            *(pltpu.VMEM(one.shape, BF16) for one in split), *operands,
        ],
        compiler_params=PARAMS,
        cost_estimate=cost(22, width),
        name="odd_whole",
    )(new_right, next_left, bond_gates)

    mine = jnp.stack([even_weight[0, 0], odd_weight[0, 0]])
    theirs = lax.ppermute(mine, "c", [(0, 1), (1, 0)])
    chip = jnp.where(c == 0, jnp.stack([mine, theirs]), jnp.stack([theirs, mine]))
    table = lax.all_to_all(jnp.broadcast_to(chip, (2 * zs, 2, 2)), ("z", "xh"), 0, 0, tiled=True)

    from_beside = lax.ppermute(other, everywhere, beside)
    from_onward = lax.ppermute(own_right, everywhere, onward)
    from_across = lax.ppermute(other_right, everywhere, across)
    is_first = pair == 0
    first = jnp.where(is_first, from_onward, from_across)
    second = jnp.where(is_first, own_left, from_beside[0])
    third = jnp.where(is_first, own_right, from_beside[1])
    fourth = jnp.where(is_first, from_beside[0], own_left)
    state = jnp.swapaxes(jnp.stack([first, second, third, fourth]), 1, 2)

    table = table.reshape(zs, 2, 2, 2)
    ordered = jnp.stack([table[:, :, 0], table[:, ::-1, 1]], axis=1).reshape(-1)
    count = ordered.shape[0]
    start = sites * (2 * lax.axis_index("z") + c)
    taken = jnp.arange(count)[None, :] <= start + jnp.arange(sites)[:, None]
    profile = jnp.sum(jnp.where(taken, ordered[None, :], 0.0), axis=1) / count
    return state, profile


def solution(mesh):
    chain, bond = mesh.shape["chain"], mesh.shape["bond"]
    fine = Mesh(mesh.devices.reshape(chain // 2, 2, bond // 4, 2, 2), ("z", "c", "y", "xh", "xl"))
    rows, columns = ("z", "c"), ("y", "xh", "xl")
    return jax.shard_map(
        per_device,
        mesh=fine,
        in_specs=(P(rows, columns, None, None), P(rows, None, None)),
        out_specs=(P(rows, columns, None, None), P(rows)),
        check_vma=False,
    )
```

```python
import functools
import math

import jax
import jax.numpy as jnp
from jax import lax
from jax.experimental import pallas as pl
from jax.experimental.pallas import tpu as pltpu
from jax.sharding import Mesh, PartitionSpec as P


EPS = 1e-06
F32, BF16 = jnp.float32, jnp.bfloat16
ROWS_CHUNK = 16


def halves(value):
    high = value.astype(BF16)
    return high, (value - high.astype(F32)).astype(BF16)


def put(high_ref, low_ref, at, value):
    high_ref[at], low_ref[at] = halves(value)


def product(lefts, rights, transposed=False):
    lhs = jnp.concatenate([part for high, low in lefts for part in (high, high, low)], axis=1)
    axis = 1 if transposed else 0
    rhs = jnp.concatenate([part for high, low in rights for part in (high, low, high)], axis=axis)
    return lax.dot_general(lhs, rhs, (((1,), (axis,)), ((), ())), preferred_element_type=F32)


def two_site_matrix(gate_ref, site, left, right, theta, phi_high, phi_low):
    width = theta.shape[2]
    for t in range(2):
        both = product([left], [right[t]])
        theta[0, t], theta[1, t] = both[:width], both[width:]
    scale = 1.0 / math.sqrt(width)
    gate = [[gate_ref[site, i, j] * scale for j in range(4)] for i in range(4)]

    def chunk(k, _):
        at = pl.ds(pl.multiple_of(k * ROWS_CHUNK, ROWS_CHUNK), ROWS_CHUNK)
        parts = [theta[u, v, at] for u in range(2) for v in range(2)]
        for s in range(2):
            for t in range(2):
                row = gate[2 * s + t]
                mixed = row[0] * parts[0] + row[1] * parts[1] + (row[2] * parts[2] + row[3] * parts[3])
                put(phi_high, phi_low, (s, t, at), mixed)
        return 0

    lax.fori_loop(0, width // ROWS_CHUNK, chunk, 0, unroll=4)


def projected(right, phi_high, phi_low, flipped, flip_high, flip_low):
    for s in range(2):
        flipped[s] = product(right, [(phi_high[s, t], phi_low[s, t]) for t in range(2)], True)
        put(flip_high, flip_low, s, flipped[s])


def orthogonalizer(flipped, flip_high, flip_low):
    width = flipped.shape[1]
    total = jnp.sum(flipped[0] * flipped[0] + flipped[1] * flipped[1], axis=(0, 1), keepdims=True)
    norm = jnp.sqrt(total + EPS)
    pairs = [(flip_high[s], flip_low[s]) for s in range(2)]
    gram = product(pairs, pairs, True) * (1.0 / (total + EPS))
    rows = lax.broadcasted_iota(jnp.int32, (width, width), 0)
    columns = lax.broadcasted_iota(jnp.int32, (width, width), 1)
    unit = jnp.where(rows == columns, 1.0, 0.0).astype(F32)
    g = halves(gram)
    square = product([g], [g])
    a = halves(square)
    two = product([a], [halves(0.0625 * square - 0.5625 * gram)])
    two = two + (2.25 * unit - 2.4375 * gram + 1.6875 * square)
    w = halves(two)
    once = product([g], [w])
    twice = product([w], [w])
    three = 1.5 * two - 0.5 * product([halves(once)], [halves(twice)])
    return three * (1.0 / norm)


def carried_planes(p, flip_high, flip_low, phi_high, phi_low, carried):
    size = carried.shape[1] * carried.shape[2] * 2
    total = jnp.zeros((1, 1), F32)
    for t in range(2):
        mixed = product(
            [(flip_high[s], flip_low[s]) for s in range(2)],
            [(phi_high[s, t], phi_low[s, t]) for s in range(2)],
        )
        plane = product([p], [halves(mixed)])
        carried[t] = plane
        total = total + jnp.sum(plane * plane, axis=(0, 1), keepdims=True)
    return jnp.sqrt(total * (1.0 / size) + EPS)


def pair_of_bond():
    return lax.axis_index("xh") ^ lax.axis_index("c")


def in_lane(value, lane, shape):
    return jnp.where(lax.broadcasted_iota(jnp.int32, shape, 1) == lane, value, 0.0)


def even_first(
    got, gates, new_left, p_out, flip_high, flip_low, phi_high, phi_low, theta, flipped, left_high, left_low, right_high, right_low
):
    width = theta.shape[2]
    for s in range(2):
        put(left_high, left_low, pl.ds(s * width, width), got[:, 0, s].reshape(width, width))
        put(right_high, right_low, s, got[:, 1, s].reshape(width, width))
    right = [(right_high[t], right_low[t]) for t in range(2)]
    two_site_matrix(gates, 2 * pair_of_bond(), (left_high[...], left_low[...]), right, theta, phi_high, phi_low)
    projected(right, phi_high, phi_low, flipped, flip_high, flip_low)
    p = orthogonalizer(flipped, flip_high, flip_low)
    p_out[...] = p
    p = halves(p)
    for s in range(2):
        new_left[s] = math.sqrt(2 * width) * product([halves(flipped[s].T)], [p])


def even_second(p_in, flip_high, flip_low, phi_high, phi_low, new_right, weight):
    norm = carried_planes(halves(p_in[...]), flip_high, flip_low, phi_high, phi_low, new_right)
    for t in range(2):
        new_right[t] = new_right[t] * (1.0 / norm)
    weight[...] = in_lane(jnp.log(norm), 0, weight.shape)


def odd_whole(
    left_in, right_in, gates, even_weight, own_left, own_right, other, other_right, weight,
    theta, flipped, carried, flip_high, flip_low, phi_high, phi_low, left_high, left_low, right_high, right_low,
):
    width = theta.shape[2]
    depth = own_left.shape[1]
    for s in range(2):
        put(left_high, left_low, pl.ds(s * width, width), left_in[s])
        put(right_high, right_low, s, right_in[s])
    right = [(right_high[t], right_low[t]) for t in range(2)]
    two_site_matrix(gates, 2 * pair_of_bond() + 1, (left_high[...], left_low[...]), right, theta, phi_high, phi_low)
    projected(right, phi_high, phi_low, flipped, flip_high, flip_low)
    y, xh, xl = lax.axis_index("y"), lax.axis_index("xh"), lax.axis_index("xl")
    blocks = [pl.ds(pl.multiple_of(b * depth, depth), depth) for b in (4 * y + 2 * xh + xl, 4 * y + 2 * (1 - xh) + (1 - xl))]
    picked = [
        tuple(jnp.concatenate([ref[s, t, at] for at in blocks for s in range(2)], axis=0) for ref in (phi_high, phi_low))
        for t in range(2)
    ]
    some = product(picked, right, True)
    p = halves(orthogonalizer(flipped, flip_high, flip_low))
    norm = carried_planes(p, flip_high, flip_low, phi_high, phi_low, carried)
    weight[...] = even_weight[...] + in_lane(jnp.log(norm), 1, weight.shape)
    some = math.sqrt(2 * width) * product([halves(some)], [p])
    inverse = 1.0 / norm
    for s in range(2):
        own_left[s] = some[s * depth : (s + 1) * depth]
        other[0, s] = some[(2 + s) * depth : (3 + s) * depth]
        own_right[s] = carried[s, blocks[0]] * inverse
        there = carried[s, blocks[1]] * inverse
        other[1, s] = there
        other_right[s] = there


def counted(sites, out):
    c = lax.axis_index("c")
    row = lax.broadcasted_iota(jnp.int32, out.shape[2:], 0)
    lane = lax.broadcasted_iota(jnp.int32, out.shape[2:], 1)
    place = sites * (2 * (row >> 1) + c) + 2 * ((row & 1) ^ c) + lane
    for side in range(2):
        block = sites * (2 * lax.axis_index("z") + (c ^ side))
        for k in range(sites):
            out[side, k] = jnp.where((lane < 2) & (place <= block + k), 1.0, 0.0)


def partial_sums(table, taken, kept, given):
    values = table[:, 0, :]
    for side, out in enumerate((kept, given)):
        sums = jnp.zeros(out.shape, F32)
        for k in range(taken.shape[1]):
            total = jnp.sum(values * taken[side, k], axis=(0, 1), keepdims=True)
            sums = sums + in_lane(total, k, out.shape)
        out[...] = sums


def assembled(own_left, own_right, beside, onward, across, state):
    def store(*sources):
        for site, source in enumerate(sources):
            for s in range(2):
                state[site, :, s, :] = source[s]

    @pl.when(pair_of_bond() == 0)
    def _():
        store(onward, own_left, own_right, beside.at[0])

    @pl.when(pair_of_bond() == 1)
    def _():
        store(across, beside.at[0], beside.at[1], own_left)


def planes(width, dtype, *lead):
    return pltpu.VMEM((*lead, width, width), dtype)


def shaped(dtype, *shape):
    return jax.ShapeDtypeStruct(shape, dtype)


VMEM = pl.BlockSpec(memory_space=pltpu.VMEM)
SMEM = pl.BlockSpec(memory_space=pltpu.SMEM)
PARAMS = pltpu.CompilerParams(vmem_limit_bytes=24 << 20)


def cost(products, width):
    return pl.CostEstimate(flops=6 * products * width**3, bytes_accessed=1 << 21, transcendentals=0)


def per_device(site_tensors, bond_gates):
    sites, depth, spins, width = site_tensors.shape
    zs, ys = lax.axis_size("z"), lax.axis_size("y")
    c = lax.axis_index("c")
    chain, bond = ("z", "c"), ("y", "xh", "xl")
    split = [
        shaped(BF16, 2, width, width), shaped(BF16, 2, width, width),
        shaped(BF16, 2, 2, width, width), shaped(BF16, 2, 2, width, width),
    ]
    operands = [
        pltpu.VMEM((2 * width, width), BF16), pltpu.VMEM((2 * width, width), BF16),
        planes(width, BF16, 2), planes(width, BF16, 2),
    ]

    by_spin = jnp.swapaxes(site_tensors, 1, 2)
    by_spin = jnp.where(c == 0, by_spin, jnp.roll(by_spin, 2, axis=0)).reshape(2, 2, spins, depth, width)
    sent = jnp.broadcast_to(by_spin[None, :, None], (ys, 2, 2, 2, spins, depth, width))
    got = lax.all_to_all(sent.reshape(-1, 2, spins, depth, width), bond, 0, 0, tiled=True)

    new_left, p, *kept = pl.pallas_call(
        even_first,
        out_shape=[shaped(F32, 2, width, width), shaped(F32, width, width), *split],
        in_specs=[VMEM, SMEM],
        out_specs=[VMEM] * 6,
        scratch_shapes=[planes(width, F32, 2, 2), planes(width, F32, 2), *operands],
        compiler_params=PARAMS,
        cost_estimate=cost(17, width),
        name="even_first",
    )(got, bond_gates)

    def number(z, k, y, i, j):
        return (((z * 2 + k) * ys + y) * 2 + i) * 2 + j

    every = [(z, k, y, i, j) for z in range(zs) for k in range(2) for y in range(ys) for i in range(2) for j in range(2)]
    route, beside, onward, across = [], [], [], []
    for z, k, y, i, j in every:
        after = ((z + k) % zs, 1 - k)
        here = number(z, k, y, i, j)
        opposite = number(z, k, y, 1 - i, 1 - j)
        beside.append((here, opposite))
        if i ^ k:
            route.append((number(*after, y, i, j), here))
            onward.append((here, number(*after, y, i, j)))
            across.append((here, number(*after, y, 1 - i, 1 - j)))
        else:
            route.append((opposite, here))
    everywhere = chain + bond
    next_left = lax.ppermute(new_left, everywhere, route)

    new_right, even_weight = pl.pallas_call(
        even_second,
        out_shape=[shaped(F32, 2, width, width), shaped(F32, 1, 128)],
        in_specs=[VMEM] * 5,
        out_specs=[VMEM] * 2,
        compiler_params=PARAMS,
        cost_estimate=cost(6, width),
        name="even_second",
    )(p, *kept)

    block = (2, depth, width)
    own_left, own_right, other, other_right, weights = pl.pallas_call(
        odd_whole,
        out_shape=[shaped(F32, *block), shaped(F32, *block), shaped(F32, 2, *block), shaped(F32, *block), shaped(F32, 1, 128)],
        in_specs=[VMEM, VMEM, SMEM, VMEM],
        out_specs=[VMEM] * 5,
        scratch_shapes=[
            planes(width, F32, 2, 2), planes(width, F32, 2), planes(width, F32, 2),
            *(pltpu.VMEM(one.shape, BF16) for one in split), *operands,
        ],
        compiler_params=PARAMS,
        cost_estimate=cost(22, width),
        name="odd_whole",
    )(new_right, next_left, bond_gates, even_weight)

    table = lax.all_to_all(jnp.broadcast_to(weights, (2 * zs, 1, 128)), ("z", "xh"), 0, 0, tiled=True)
    from_beside = lax.ppermute(other, everywhere, beside)
    from_onward = lax.ppermute(own_right, everywhere, onward)
    from_across = lax.ppermute(other_right, everywhere, across)
    taken = pl.pallas_call(
        functools.partial(counted, sites),
        out_shape=shaped(F32, 2, sites, 2 * zs, 128),
        out_specs=VMEM,
        compiler_params=PARAMS,
        name="counted",
    )()
    kept_sums, given_sums = pl.pallas_call(
        partial_sums,
        out_shape=[shaped(F32, 1, 128)] * 2,
        in_specs=[VMEM] * 2,
        out_specs=[VMEM] * 2,
        compiler_params=PARAMS,
        name="partial_sums",
    )(table, taken)
    taken_sums = lax.ppermute(given_sums, "c", [(0, 1), (1, 0)])
    profile = (kept_sums + taken_sums)[0, :sites] / (sites * 2 * zs)
    state = pl.pallas_call(
        assembled,
        out_shape=shaped(F32, *site_tensors.shape),
        in_specs=[VMEM] * 5,
        out_specs=VMEM,
        compiler_params=PARAMS,
        name="assembled",
    )(own_left, own_right, from_beside, from_onward, from_across)
    return state, profile


def solution(mesh):
    chain, bond = mesh.shape["chain"], mesh.shape["bond"]
    fine = Mesh(mesh.devices.reshape(chain // 2, 2, bond // 4, 2, 2), ("z", "c", "y", "xh", "xl"))
    rows, columns = ("z", "c"), ("y", "xh", "xl")

    return jax.shard_map(
        per_device,
        mesh=fine,
        in_specs=(P(rows, columns, None, None), P(rows, None, None)),
        out_specs=(P(rows, columns, None, None), P(rows)),
        check_vma=False,
    )
```
